32 devices in a mesh: row: 4 (over y, core), col: 8 (over z, x).
Axes of the slice: x: 2, y: 2, z: 4, core: 2. Of those that a mesh axis runs over, the one named last changes fastest.
Arguments:
- amplitudes: float32 [16, 16, 768, 768], P('row', 'col'), may hold values from -0.6 to 0.6
- integrals: float32 [16, 16, 768, 768], P('row', 'col'), may hold values from -6 to 6
- factors: float32 [16, 2048, 768], P('col', 'row'), may hold values from -0.21 to 0.21
- occ_energy: float32 [16], replicated, may hold values from -2 to -0.5
- vir_energy: float32 [768], replicated, may hold values from 0.5 to 3
Outputs:
- new_amplitudes: float32 [16, 16, 768, 768], P('row', 'col')
The draws below stay inside these ranges and needn't reach their ends.
All inputs are finite; a program needn't handle non-finite values.
Results may differ from the reference program's by a relative error of at most 0.00005.
Values sent between devices are 32-bit elements; how exact they have to be, the bound alone decides.
A program may use at most 192 MiB of HBM per device.

```python
import jax
import jax.numpy as jnp
from jax import lax

O = 16
V = 768
NAUX = 2048


def steps_of(stream_key, extent, shards, smallest, largest):
    gain = 1.0
    for axis_at, parts in shards:
        draws = jax.random.uniform(jax.random.fold_in(jax.random.fold_in(stream_key, 6), axis_at), (parts,), jnp.float32, smallest / len(shards), largest / len(shards))
        gain = gain * jnp.repeat(jnp.exp(draws), extent[axis_at] // parts).reshape((-1,) + (1,) * (len(extent) - 1 - axis_at))
    return gain


def centred(key, shape, width, limit, shards=(), kind=jnp.bfloat16):
    factor_of = steps_of(key, shape, shards, -0.22, 0.18) if shards else 1.0
    array = jax.random.normal(key, shape, jnp.float32) * width * factor_of
    return jnp.minimum(jnp.maximum(array, -limit), limit).astype(kind)


def setup_inputs(seed: int = 0) -> dict:
    key_list = jax.random.split(jax.random.key(seed), 6)
    amplitudes = centred(key_list[0], (O, O, V, V), 0.1, 0.6, ((0, 4), (1, 8)), jnp.float32)
    integrals = centred(key_list[1], (O, O, V, V), 1.0, 6.0, ((0, 4), (1, 8)), jnp.float32)
    factors = centred(key_list[2], (O, NAUX, V), 0.03, 0.21, ((0, 8), (1, 4)), jnp.float32)
    occ_energy = jnp.clip(jax.random.uniform(key_list[3], (O,), jnp.float32, -2.0, -0.5), -2.0, -0.5)
    vir_energy = jnp.clip(jax.random.uniform(key_list[4], (V,), jnp.float32, 0.5, 3.0), 0.5, 3.0)
    return {"amplitudes": amplitudes, "integrals": integrals, "factors": factors, "occ_energy": occ_energy, "vir_energy": vir_energy}


def reference(amplitudes, integrals, factors, occ_energy, vir_energy):
    exact = lax.Precision.HIGHEST

    def one_row(occ_index):
        row_tiles = amplitudes[occ_index]
        col_tiles = jnp.swapaxes(amplitudes[:, occ_index], 1, 2)
        combined = 2.0 * row_tiles - col_tiles
        return jnp.einsum("jab,jpb->pa", combined, factors, precision=exact)

    summed = lax.map(one_row, jnp.arange(O, dtype=jnp.int32))

    def out_row(occ_index):
        direct = jnp.einsum("pa,jpb->jab", summed[occ_index], factors, precision=exact)
        mirror = jnp.einsum("pa,jpb->jab", factors[occ_index], summed, precision=exact)
        denominator = (occ_energy[occ_index] + occ_energy[:, None, None]
                       - vir_energy[None, :, None] - vir_energy[None, None, :])
        return (integrals[occ_index] + direct + mirror) / denominator

    return lax.map(out_row, jnp.arange(O, dtype=jnp.int32))
```

```python
import functools

import jax
import jax.numpy as jnp
from jax import lax
from jax.experimental import pallas as pl
from jax.experimental.pallas import tpu as pltpu
from jax.sharding import PartitionSpec as P

VMEM_LIMIT = 63 * 1024 * 1024
NN = (((1,), (0,)), ((), ()))
NT = (((1,), (1,)), ((), ()))
TN = (((0,), (0,)), ((), ()))


def split(x):
    hi = x.astype(jnp.bfloat16)
    return hi, (x - hi.astype(jnp.float32)).astype(jnp.bfloat16)


def dot3(lhs, rhs, dims):
    mul = functools.partial(lax.dot_general, dimension_numbers=dims, preferred_element_type=jnp.float32)
    return mul(lhs[0], rhs[0]) + (mul(lhs[0], rhs[1]) + mul(lhs[1], rhs[0]))


def left_kernel(tile, oj, vir, t_ref, l_ref, x_ref, hi_ref, lo_ref):
    @pl.when(pl.program_id(1) == 0)
    def _():
        for j in range(oj):
            hi, lo = split(t_ref[0, j])
            hi_ref[:, j * vir:(j + 1) * vir] = hi
            lo_ref[:, j * vir:(j + 1) * vir] = lo

    @pl.loop(0, x_ref.shape[0] // tile)
    def _(step):
        rows = pl.ds(step * tile, tile)
        x_ref[rows, :] = dot3(split(l_ref[rows, :]), (hi_ref[...], lo_ref[...]), NT)


def left_product(amplitudes, factors):
    oi, oj, vir, _ = amplitudes.shape
    aux = factors.shape[0]
    block = min(512, aux)
    return pl.pallas_call(
        functools.partial(left_kernel, min(256, block), oj, vir),
        grid=(oi, aux // block),
        in_specs=[
            pl.BlockSpec((1, oj, vir, vir), lambda i, p: (i, 0, 0, 0)),
            pl.BlockSpec((block, oj * vir), lambda i, p: (p, 0)),
        ],
        out_specs=pl.BlockSpec((block, vir), lambda i, p: (p, i)),
        out_shape=jax.ShapeDtypeStruct((aux, oi * vir), jnp.float32),
        scratch_shapes=[pltpu.VMEM((vir, oj * vir), jnp.bfloat16)] * 2,
        compiler_params=pltpu.CompilerParams(vmem_limit_bytes=VMEM_LIMIT),
        cost_estimate=pl.CostEstimate(flops=6 * oi * oj * vir * vir * aux, bytes_accessed=4 * (oi * oj * vir * vir + aux * oi * (oj + 1) * vir), transcendentals=0),
        name="left_product",
    )(amplitudes, factors)


def right_kernel(tile, oi, vir, t_ref, l_ref, y_ref, hi_ref, lo_ref):
    @pl.when(pl.program_id(1) == 0)
    def _():
        for i in range(oi):
            hi, lo = split(t_ref[i, 0])
            hi_ref[i * vir:(i + 1) * vir, :] = hi
            lo_ref[i * vir:(i + 1) * vir, :] = lo

    @pl.loop(0, y_ref.shape[0] // tile)
    def _(step):
        rows = pl.ds(step * tile, tile)
        y_ref[rows, :] = dot3(split(l_ref[rows, :]), (hi_ref[...], lo_ref[...]), NN)


def right_product(amplitudes, factors):
    oi, oj, vir, _ = amplitudes.shape
    aux = factors.shape[0]
    block = min(256, aux)
    return pl.pallas_call(
        functools.partial(right_kernel, min(256, block), oi, vir),
        grid=(oj, aux // block),
        in_specs=[
            pl.BlockSpec((oi, 1, vir, vir), lambda j, p: (0, j, 0, 0)),
            pl.BlockSpec((block, oi * vir), lambda j, p: (p, 0)),
        ],
        out_specs=pl.BlockSpec((block, vir), lambda j, p: (p, j)),
        out_shape=jax.ShapeDtypeStruct((aux, oj * vir), jnp.float32),
        scratch_shapes=[pltpu.VMEM((oi * vir, vir), jnp.bfloat16)] * 2,
        compiler_params=pltpu.CompilerParams(vmem_limit_bytes=VMEM_LIMIT),
        cost_estimate=pl.CostEstimate(flops=6 * oi * oj * vir * vir * aux, bytes_accessed=4 * (oi * oj * vir * vir + aux * oj * (oi + 1) * vir), transcendentals=0),
        name="right_product",
    )(amplitudes, factors)


def final_kernel(left_ref, right_ref, vir_row_ref, vir_col_ref, k_ref, sr_ref, lc_ref, lr_ref, sc_ref, out_ref, acc_ref):
    i, j, step = pl.program_id(0), pl.program_id(1), pl.program_id(2)

    @pl.when(step == 0)
    def _():
        acc_ref[...] = k_ref[0, 0]

    acc_ref[...] += dot3(split(sr_ref[...]), split(lc_ref[...]), TN) + dot3(split(lr_ref[...]), split(sc_ref[...]), TN)

    @pl.when(step == pl.num_programs(2) - 1)
    def _():
        pair = left_ref[i] + right_ref[j]
        out_ref[0, 0] = acc_ref[...] / (pair - vir_col_ref[...] - vir_row_ref[...])


def final(integrals, sum_row, fac_col, fac_row, sum_col, occ_left, occ_right, vir_energy):
    oi, oj, vir, _ = integrals.shape
    aux = sum_row.shape[0]
    block = min(512, aux)
    pair = pl.BlockSpec((1, 1, vir, vir), lambda i, j, p: (i, j, 0, 0))
    row = pl.BlockSpec((block, vir), lambda i, j, p: (p, i))
    col = pl.BlockSpec((block, vir), lambda i, j, p: (p, j))
    smem = pl.BlockSpec(memory_space=pltpu.SMEM)
    return pl.pallas_call(
        final_kernel,
        grid=(oi, oj, aux // block),
        in_specs=[
            smem,
            smem,
            pl.BlockSpec((1, vir), lambda i, j, p: (0, 0)),
            pl.BlockSpec((vir, 1), lambda i, j, p: (0, 0)),
            pair, row, col, row, col,
        ],
        out_specs=pair,
        out_shape=jax.ShapeDtypeStruct(integrals.shape, jnp.float32),
        scratch_shapes=[pltpu.VMEM((vir, vir), jnp.float32)],
        compiler_params=pltpu.CompilerParams(vmem_limit_bytes=VMEM_LIMIT),
        name="final",
    )(occ_left, occ_right, vir_energy[None, :], vir_energy[:, None], integrals, sum_row, fac_col, fac_row, sum_col)


def pick(pieces, index):
    return lax.dynamic_index_in_dim(pieces, index, 0, keepdims=False)


def to_row(shard, rows, cols):
    ratio = cols // rows
    col = lax.axis_index("col")
    parts = shard.reshape(ratio, shard.shape[0] // ratio, shard.shape[1])
    got = []
    for k in range(ratio):
        perm = [
            (r * cols + c, (c // ratio) * cols + r * ratio + (c + k) % ratio)
            for r in range(rows) for c in range(cols)
        ]
        got.append(lax.ppermute(pick(parts, lax.rem(col + k, ratio)), ("row", "col"), perm))
    got = jnp.stack(got)
    return jnp.concatenate([pick(got, lax.rem(col + ratio - m, ratio)) for m in range(ratio)], axis=1)


def to_col(shard, rows, cols):
    ratio = cols // rows
    col = lax.axis_index("col")
    parts = jnp.stack(jnp.split(shard, ratio, axis=1))
    got = []
    for k in range(ratio):
        perm = [
            ((c // ratio) * cols + r * ratio + (c + k) % ratio, r * cols + c)
            for r in range(rows) for c in range(cols)
        ]
        got.append(lax.ppermute(pick(parts, lax.rem(col + ratio - k, ratio)), ("row", "col"), perm))
    got = jnp.stack(got)
    return jnp.concatenate([pick(got, lax.rem(m + ratio - lax.rem(col, ratio), ratio)) for m in range(ratio)], axis=0)


def shards(rows, cols, amplitudes, integrals, factors, occ_energy, vir_energy):
    oi, oj, vir, _ = amplitudes.shape
    own = jnp.transpose(factors, (1, 0, 2)).reshape(factors.shape[1], oj * vir)
    fac_col = lax.all_gather(own, "row", axis=0, tiled=True)
    fac_row = lax.all_gather(to_row(own, rows, cols), "col", axis=0, tiled=True)
    left = lax.psum_scatter(left_product(amplitudes, fac_col), "col", scatter_dimension=0, tiled=True)
    right = lax.psum_scatter(right_product(amplitudes, fac_row), "row", scatter_dimension=0, tiled=True)
    summed = 2.0 * left - to_row(right, rows, cols)
    sum_row = lax.all_gather(summed, "col", axis=0, tiled=True)
    sum_col = lax.all_gather(to_col(summed, rows, cols), "row", axis=0, tiled=True)
    occ_left = lax.dynamic_slice_in_dim(occ_energy, lax.axis_index("row") * oi, oi)
    occ_right = lax.dynamic_slice_in_dim(occ_energy, lax.axis_index("col") * oj, oj)
    return final(integrals, sum_row, fac_col, fac_row, sum_col, occ_left, occ_right, vir_energy)


def solution(mesh):
    return jax.shard_map(
        functools.partial(shards, mesh.shape["row"], mesh.shape["col"]),
        mesh=mesh,
        in_specs=(
            P("row", "col", None, None),
            P("row", "col", None, None),
            P("col", "row", None),
            P(),
            P(),
        ),
        out_specs=P("row", "col", None, None),
        check_vma=False,
    )
```

```python
import functools

import jax
import jax.numpy as jnp
from jax import lax
from jax.experimental import pallas as pl
from jax.experimental.pallas import tpu as pltpu
from jax.sharding import PartitionSpec as P


VMEM_LIMIT = 63 * 1024 * 1024
NN = (((1,), (0,)), ((), ()))
NT = (((1,), (1,)), ((), ()))
TN = (((0,), (0,)), ((), ()))


def split(x):
    hi = x.astype(jnp.bfloat16)
    return hi, (x - hi.astype(jnp.float32)).astype(jnp.bfloat16)


def dot3(lhs, rhs, dims):
    mul = functools.partial(lax.dot_general, dimension_numbers=dims, preferred_element_type=jnp.float32)
    return mul(lhs[0], rhs[0]) + (mul(lhs[0], rhs[1]) + mul(lhs[1], rhs[0]))


def left_kernel(tile, oj, vir, t_ref, l_ref, x_ref, hi_ref, lo_ref):
    @pl.when(pl.program_id(1) == 0)
    def _():
        for j in range(oj):
            hi, lo = split(t_ref[0, j])
            hi_ref[:, j * vir:(j + 1) * vir] = hi
            lo_ref[:, j * vir:(j + 1) * vir] = lo

    @pl.loop(0, x_ref.shape[0] // tile)
    def _(step):
        rows = pl.ds(step * tile, tile)
        x_ref[rows, :] = dot3(split(l_ref[rows, :]), (hi_ref[...], lo_ref[...]), NT)


def left_product(amplitudes, factors, part, parts):
    oi, oj, vir, _ = amplitudes.shape
    aux = factors.shape[0]
    block = min(512, aux)
    own = oi // parts
    return pl.pallas_call(
        functools.partial(left_kernel, min(256, block), oj, vir),
        grid=(own, aux // block),
        in_specs=[
            pl.BlockSpec((1, oj, vir, vir), lambda i, p: (part * own + i, 0, 0, 0)),
            pl.BlockSpec((block, oj * vir), lambda i, p: (p, 0)),
        ],
        out_specs=pl.BlockSpec((block, vir), lambda i, p: (p, i)),
        out_shape=jax.ShapeDtypeStruct((aux, own * vir), jnp.float32),
        scratch_shapes=[pltpu.VMEM((vir, oj * vir), jnp.bfloat16)] * 2,
        compiler_params=pltpu.CompilerParams(vmem_limit_bytes=VMEM_LIMIT),
        cost_estimate=pl.CostEstimate(flops=6 * own * oj * vir * vir * aux, bytes_accessed=4 * (own * oj * vir * vir + aux * own * (oj + 1) * vir), transcendentals=0),
        name="left_product",
    )(amplitudes, factors)


def right_kernel(oi, vir, parts, t_ref, *refs):
    l_refs, (y_ref, hi_ref, lo_ref) = refs[:parts], refs[parts:]

    @pl.when(pl.program_id(1) == 0)
    def _():
        for i in range(oi):
            hi, lo = split(t_ref[i, 0])
            hi_ref[i * vir:(i + 1) * vir, :] = hi
            lo_ref[i * vir:(i + 1) * vir, :] = lo

    total = 0.0
    for part, l_ref in enumerate(l_refs):
        wide = l_ref.shape[1]
        rows = slice(part * wide, (part + 1) * wide)
        total = total + dot3(split(l_ref[...]), (hi_ref[rows, :], lo_ref[rows, :]), NN)
    y_ref[...] = total


def right_product(amplitudes, factors, rows, piece, pieces):
    oi, oj, vir, _ = amplitudes.shape
    aux = factors[0].shape[0]
    block = aux // (rows * pieces)
    parts = len(factors)
    wide = factors[0].shape[1]
    return pl.pallas_call(
        functools.partial(right_kernel, oi, vir, parts),
        grid=(oj, rows),
        in_specs=[pl.BlockSpec((oi, 1, vir, vir), lambda j, p: (0, j, 0, 0))]
        + [pl.BlockSpec((block, wide), lambda j, p: (p * pieces + piece, 0))] * parts,
        out_specs=pl.BlockSpec((block, vir), lambda j, p: (p, j)),
        out_shape=jax.ShapeDtypeStruct((rows * block, oj * vir), jnp.float32),
        scratch_shapes=[pltpu.VMEM((oi * vir, vir), jnp.bfloat16)] * 2,
        compiler_params=pltpu.CompilerParams(vmem_limit_bytes=VMEM_LIMIT),
        cost_estimate=pl.CostEstimate(flops=6 * oi * oj * vir * vir * rows * block, bytes_accessed=4 * (oi * oj * vir * vir + rows * block * oj * (oi + 1) * vir), transcendentals=0),
        name="right_product",
    )(amplitudes, *factors)


def base_kernel(k_ref, lr_ref, sc_ref, *refs):
    out_ref = refs[-1]
    step = pl.program_id(2)
    term = dot3(split(lr_ref[...]), split(sc_ref[...]), TN)

    @pl.when(step == 0)
    def _():
        out_ref[0, 0] = k_ref[0, 0] + term

    @pl.when(step > 0)
    def _():
        out_ref[0, 0] += term


def final_kernel(first, left_ref, right_ref, vir_row_ref, vir_col_ref, k_ref, sr_ref, lc_ref, *refs):
    out_ref, acc_ref = refs[-2:]
    i, j, step = pl.program_id(0), pl.program_id(1), pl.program_id(2)

    @pl.when(step == 0)
    def _():
        acc_ref[...] = k_ref[0, 0]

    acc_ref[...] += dot3(split(sr_ref[...]), split(lc_ref[...]), TN)

    @pl.when(step == pl.num_programs(2) - 1)
    def _():
        pair = left_ref[first + i] + right_ref[j]
        out_ref[0, 0] = acc_ref[...] / (pair - vir_col_ref[...] - vir_row_ref[...])


def tile_call(kernel, shape, aux, part, parts, block, lead, pair_in, row_in, col_in, earlier, in_place, scratch):
    oi, oj, vir, _ = shape
    own = oi // parts
    first = part * own
    pair = pl.BlockSpec((1, 1, vir, vir), lambda i, j, p: (first + i, j, 0, 0))
    args = [array for array, _ in lead] + [pair_in, row_in, col_in]
    specs = [spec for _, spec in lead] + [
        pair,
        pl.BlockSpec((block, vir), lambda i, j, p: (p, i)),
        pl.BlockSpec((block, vir), lambda i, j, p: (p, j)),
    ]
    alias = {len(lead): 0} if in_place else {}
    if earlier is not None:
        alias = {len(args): 0}
        args.append(earlier)
        specs.append(pl.BlockSpec(memory_space=pl.ANY))
    return pl.pallas_call(
        kernel,
        grid=(own, oj, aux // block),
        in_specs=specs,
        out_specs=pair,
        out_shape=jax.ShapeDtypeStruct(shape, jnp.float32),
        input_output_aliases=alias,
        scratch_shapes=scratch,
        compiler_params=pltpu.CompilerParams(vmem_limit_bytes=VMEM_LIMIT),
        cost_estimate=pl.CostEstimate(flops=6 * own * oj * vir * vir * aux, bytes_accessed=4 * own * oj * (2 * vir * vir + 2 * aux * vir), transcendentals=0),
    )(*args)


def base(integrals, fac_row, sum_col, part, parts, earlier):
    aux = fac_row.shape[0]
    return tile_call(base_kernel, integrals.shape, aux, part, parts, min(1024, aux), [], integrals, fac_row, sum_col, earlier, False, [])


def final(so_far, sum_row, fac_col, occ_left, occ_right, vir_energy, part, parts):
    oi, _, vir, _ = so_far.shape
    aux = sum_row.shape[0]
    smem = pl.BlockSpec(memory_space=pltpu.SMEM)
    lead = [
        (occ_left, smem),
        (occ_right, smem),
        (vir_energy[None, :], pl.BlockSpec((1, vir), lambda i, j, p: (0, 0))),
        (vir_energy[:, None], pl.BlockSpec((vir, 1), lambda i, j, p: (0, 0))),
    ]
    kernel = functools.partial(final_kernel, part * (oi // parts))
    return tile_call(kernel, so_far.shape, aux, part, parts, min(1024, aux), lead, so_far, sum_row, fac_col, None, True, [pltpu.VMEM((vir, vir), jnp.float32)])


def ring_of(cols):
    return list(range(0, cols, 2)) + list(range(1, cols, 2))[::-1]


def ring_facts(cols, way):
    ring = ring_of(cols)
    perm = [(ring[k], ring[(k + way) % cols]) for k in range(cols)]
    place = [ring.index(c) for c in range(cols)]
    at = jnp.asarray(place, jnp.int32)[lax.axis_index("col")]
    owner = lambda back: jnp.asarray(ring, jnp.int32)[lax.rem(at + cols - way * back + cols, cols)]
    return perm, owner


def ring_gather(shard, cols):
    half = shard.shape[0] // 2
    full = jnp.zeros((shard.shape[0] * cols, shard.shape[1]), shard.dtype)
    full = lax.dynamic_update_slice(full, shard, (lax.axis_index("col") * 2 * half, 0))
    ways = [(way, shard[k * half:(k + 1) * half], *ring_facts(cols, way)) for k, way in enumerate((1, -1))]
    held = [w[1] for w in ways]
    for step in range(1, cols):
        for k, (way, _, perm, owner) in enumerate(ways):
            held[k] = lax.ppermute(held[k], "col", perm)
        for k, (way, _, perm, owner) in enumerate(ways):
            full = lax.dynamic_update_slice(full, held[k], (owner(step) * 2 * half + k * half, 0))
    return full


def ring_scatter(array, cols):
    size = array.shape[0] // cols
    half = size // 2
    sums = []
    for k, way in enumerate((1, -1)):
        perm, owner = ring_facts(cols, way)
        mine = lambda back: lax.dynamic_slice(array, (owner(back) * size + k * half, 0), (half, array.shape[1]))
        held = mine(1)
        for step in range(1, cols):
            held = lax.ppermute(held, "col", perm)
            held = held + mine(step + 1)
        sums.append(held)
    return jnp.concatenate(sums, axis=0)


def pick(pieces, index):
    return lax.dynamic_index_in_dim(pieces, index, 0, keepdims=False)


def to_row(shard, rows, cols):
    ratio = cols // rows
    col = lax.axis_index("col")
    parts = shard.reshape(ratio, shard.shape[0] // ratio, shard.shape[1])
    got = []
    for k in range(ratio):
        perm = [
            (r * cols + c, (c // ratio) * cols + r * ratio + (c + k) % ratio)
            for r in range(rows) for c in range(cols)
        ]
        got.append(lax.ppermute(pick(parts, lax.rem(col + k, ratio)), ("row", "col"), perm))
    got = jnp.stack(got)
    return jnp.concatenate([pick(got, lax.rem(col + ratio - m, ratio)) for m in range(ratio)], axis=1)


def to_col(shard, rows, cols):
    ratio = cols // rows
    col = lax.axis_index("col")
    parts = jnp.stack(jnp.split(shard, ratio, axis=1))
    got = []
    for k in range(ratio):
        perm = [
            ((c // ratio) * cols + r * ratio + (c + k) % ratio, r * cols + c)
            for r in range(rows) for c in range(cols)
        ]
        got.append(lax.ppermute(pick(parts, lax.rem(col + ratio - k, ratio)), ("row", "col"), perm))
    got = jnp.stack(got)
    return jnp.concatenate([pick(got, lax.rem(m + ratio - lax.rem(col, ratio), ratio)) for m in range(ratio)], axis=0)


def shards(rows, cols, amplitudes, integrals, factors, occ_energy, vir_energy):
    oi, oj, vir, _ = amplitudes.shape
    parts = 2 if oi % 2 == 0 else 1
    pieces = 4
    wide = oi // parts * vir
    own = jnp.transpose(factors, (1, 0, 2)).reshape(factors.shape[1], oj * vir)
    fac_col = lax.all_gather(own, "row", axis=0, tiled=True)
    moved = to_row(own, rows, cols)
    fac_row = [ring_gather(moved[:, g * wide:(g + 1) * wide], cols) for g in range(parts)]
    left = []
    for g in range(parts):
        left.append(left_product(amplitudes, fac_col, g, parts))
    left = [ring_scatter(part, cols) for part in left]
    right = []
    for h in range(pieces):
        right.append(right_product(amplitudes, fac_row, rows, h, pieces))
    right = [lax.psum_scatter(piece, "row", scatter_dimension=0, tiled=True) for piece in right]
    right = to_row(jnp.concatenate(right, axis=0), rows, cols)
    summed = [2.0 * left[g] - right[:, g * wide:(g + 1) * wide] for g in range(parts)]
    sum_col = lax.all_gather(to_col(jnp.concatenate(summed, axis=1), rows, cols), "row", axis=0, tiled=True)
    sum_row = [ring_gather(part, cols) for part in summed]
    occ_left = lax.dynamic_slice_in_dim(occ_energy, lax.axis_index("row") * oi, oi)
    occ_right = lax.dynamic_slice_in_dim(occ_energy, lax.axis_index("col") * oj, oj)
    out = None
    for g in range(parts):
        out = base(integrals, fac_row[g], sum_col, g, parts, out)
    for g in range(parts):
        out = final(out, sum_row[g], fac_col, occ_left, occ_right, vir_energy, g, parts)
    return out


def solution(mesh):
    cols = mesh.shape["col"]
    return jax.shard_map(
        functools.partial(shards, mesh.shape["row"], cols),
        mesh=mesh,
        in_specs=(
            P("row", "col", None, None),
            P("row", "col", None, None),
            P("col", "row", None),
            P(),
            P(),
        ),
        out_specs=P("row", "col", None, None),
        check_vma=False,
    )
```

```python
import functools

import jax
import jax.numpy as jnp
from jax import lax
from jax.experimental import pallas as pl
from jax.experimental.pallas import tpu as pltpu
from jax.sharding import PartitionSpec as P


VMEM_LIMIT = 63 * 1024 * 1024
NN = (((1,), (0,)), ((), ()))
NT = (((1,), (1,)), ((), ()))
TN = (((0,), (0,)), ((), ()))


def split(x):
    hi = x.astype(jnp.bfloat16)
    return hi, (x - hi.astype(jnp.float32)).astype(jnp.bfloat16)


def dot3(lhs, rhs, dims):
    mul = functools.partial(lax.dot_general, dimension_numbers=dims, preferred_element_type=jnp.float32)
    return mul(lhs[0], rhs[0]) + (mul(lhs[0], rhs[1]) + mul(lhs[1], rhs[0]))


def left_kernel(tile, oj, vir, t_ref, l_ref, x_ref, hi_ref, lo_ref):
    @pl.when(pl.program_id(1) == 0)
    def _():
        for j in range(oj):
            hi, lo = split(t_ref[0, j])
            hi_ref[:, j * vir:(j + 1) * vir] = hi
            lo_ref[:, j * vir:(j + 1) * vir] = lo

    @pl.loop(0, x_ref.shape[0] // tile)
    def _(step):
        rows = pl.ds(step * tile, tile)
        x_ref[rows, :] = dot3(split(l_ref[rows, :]), (hi_ref[...], lo_ref[...]), NT)


def left_product(amplitudes, factors, part, parts):
    oi, oj, vir, _ = amplitudes.shape
    aux = factors.shape[0]
    block = min(512, aux)
    own = oi // parts
    return pl.pallas_call(
        functools.partial(left_kernel, min(256, block), oj, vir),
        grid=(own, aux // block),
        in_specs=[
            pl.BlockSpec((1, oj, vir, vir), lambda i, p: (part * own + i, 0, 0, 0)),
            pl.BlockSpec((block, oj * vir), lambda i, p: (p, 0)),
        ],
        out_specs=pl.BlockSpec((block, vir), lambda i, p: (p, i)),
        out_shape=jax.ShapeDtypeStruct((aux, own * vir), jnp.float32),
        scratch_shapes=[pltpu.VMEM((vir, oj * vir), jnp.bfloat16)] * 2,
        compiler_params=pltpu.CompilerParams(vmem_limit_bytes=VMEM_LIMIT),
        cost_estimate=pl.CostEstimate(flops=6 * own * oj * vir * vir * aux, bytes_accessed=4 * (own * oj * vir * vir + aux * own * (oj + 1) * vir), transcendentals=0),
        name="left_product",
    )(amplitudes, factors)


def right_kernel(oi, vir, parts, t_ref, *refs):
    l_refs, (y_ref, hi_ref, lo_ref) = refs[:parts], refs[parts:]

    @pl.when(pl.program_id(1) == 0)
    def _():
        for i in range(oi):
            hi, lo = split(t_ref[i, 0])
            hi_ref[i * vir:(i + 1) * vir, :] = hi
            lo_ref[i * vir:(i + 1) * vir, :] = lo

    total = 0.0
    for part, l_ref in enumerate(l_refs):
        wide = l_ref.shape[1]
        rows = slice(part * wide, (part + 1) * wide)
        total = total + dot3(split(l_ref[...]), (hi_ref[rows, :], lo_ref[rows, :]), NN)
    y_ref[...] = total


def right_product(amplitudes, factors, rows, piece, pieces):
    oi, oj, vir, _ = amplitudes.shape
    aux = factors[0].shape[0]
    block = aux // (rows * pieces)
    parts = len(factors)
    wide = factors[0].shape[1]
    return pl.pallas_call(
        functools.partial(right_kernel, oi, vir, parts),
        grid=(oj, rows),
        in_specs=[pl.BlockSpec((oi, 1, vir, vir), lambda j, p: (0, j, 0, 0))]
        + [pl.BlockSpec((block, wide), lambda j, p: (p * pieces + piece, 0))] * parts,
        out_specs=pl.BlockSpec((block, vir), lambda j, p: (p, j)),
        out_shape=jax.ShapeDtypeStruct((rows * block, oj * vir), jnp.float32),
        scratch_shapes=[pltpu.VMEM((oi * vir, vir), jnp.bfloat16)] * 2,
        compiler_params=pltpu.CompilerParams(vmem_limit_bytes=VMEM_LIMIT),
        cost_estimate=pl.CostEstimate(flops=6 * oi * oj * vir * vir * rows * block, bytes_accessed=4 * (oi * oj * vir * vir + rows * block * oj * (oi + 1) * vir), transcendentals=0),
        name="right_product",
    )(amplitudes, *factors)


def base_kernel(k_ref, lr_ref, sc_ref, *refs):
    out_ref = refs[-1]
    step = pl.program_id(2)
    term = dot3(split(lr_ref[...]), split(sc_ref[...]), TN)

    @pl.when(step == 0)
    def _():
        out_ref[0, 0] = k_ref[0, 0] + term

    @pl.when(step > 0)
    def _():
        out_ref[0, 0] += term


def final_kernel(first, left_ref, right_ref, vir_row_ref, vir_col_ref, k_ref, sr_ref, lc_ref, *refs):
    out_ref, acc_ref = refs[-2:]
    i, j, step = pl.program_id(0), pl.program_id(1), pl.program_id(2)

    @pl.when(step == 0)
    def _():
        acc_ref[...] = k_ref[0, 0]

    acc_ref[...] += dot3(split(sr_ref[...]), split(lc_ref[...]), TN)

    @pl.when(step == pl.num_programs(2) - 1)
    def _():
        pair = left_ref[first + i] + right_ref[j]
        out_ref[0, 0] = acc_ref[...] / (pair - vir_col_ref[...] - vir_row_ref[...])


def tile_call(kernel, shape, aux, part, parts, block, lead, pair_in, row_in, col_in, earlier, in_place, scratch):
    oi, oj, vir, _ = shape
    own = oi // parts
    first = part * own
    pair = pl.BlockSpec((1, 1, vir, vir), lambda i, j, p: (first + i, j, 0, 0))
    args = [array for array, _ in lead] + [pair_in, row_in, col_in]
    specs = [spec for _, spec in lead] + [
        pair,
        pl.BlockSpec((block, vir), lambda i, j, p: (p, i)),
        pl.BlockSpec((block, vir), lambda i, j, p: (p, j)),
    ]
    alias = {len(lead): 0} if in_place else {}
    if earlier is not None:
        alias = {len(args): 0}
        args.append(earlier)
        specs.append(pl.BlockSpec(memory_space=pl.ANY))
    return pl.pallas_call(
        kernel,
        grid=(own, oj, aux // block),
        in_specs=specs,
        out_specs=pair,
        out_shape=jax.ShapeDtypeStruct(shape, jnp.float32),
        input_output_aliases=alias,
        scratch_shapes=scratch,
        compiler_params=pltpu.CompilerParams(vmem_limit_bytes=VMEM_LIMIT),
        cost_estimate=pl.CostEstimate(flops=6 * own * oj * vir * vir * aux, bytes_accessed=4 * own * oj * (2 * vir * vir + 2 * aux * vir), transcendentals=0),
    )(*args)


def base(integrals, fac_row, sum_col, part, parts, earlier):
    aux = fac_row.shape[0]
    return tile_call(base_kernel, integrals.shape, aux, part, parts, min(1024, aux), [], integrals, fac_row, sum_col, earlier, False, [])


def final(so_far, sum_row, fac_col, occ_left, occ_right, vir_energy, part, parts):
    oi, _, vir, _ = so_far.shape
    aux = sum_row.shape[0]
    smem = pl.BlockSpec(memory_space=pltpu.SMEM)
    lead = [
        (occ_left, smem),
        (occ_right, smem),
        (vir_energy[None, :], pl.BlockSpec((1, vir), lambda i, j, p: (0, 0))),
        (vir_energy[:, None], pl.BlockSpec((vir, 1), lambda i, j, p: (0, 0))),
    ]
    kernel = functools.partial(final_kernel, part * (oi // parts))
    return tile_call(kernel, so_far.shape, aux, part, parts, min(1024, aux), lead, so_far, sum_row, fac_col, None, True, [pltpu.VMEM((vir, vir), jnp.float32)])


def ring_of(cols):
    return list(range(0, cols, 2)) + list(range(1, cols, 2))[::-1]


def ring_facts(cols, way):
    ring = ring_of(cols)
    perm = [(ring[k], ring[(k + way) % cols]) for k in range(cols)]
    place = [ring.index(c) for c in range(cols)]
    at = jnp.asarray(place, jnp.int32)[lax.axis_index("col")]
    owner = lambda back: jnp.asarray(ring, jnp.int32)[lax.rem(at + cols - way * back + cols, cols)]
    return perm, owner


def ring_gather(shard, cols):
    half = shard.shape[0] // 2
    full = jnp.zeros((shard.shape[0] * cols, shard.shape[1]), shard.dtype)
    full = lax.dynamic_update_slice(full, shard, (lax.axis_index("col") * 2 * half, 0))
    ways = [(way, shard[k * half:(k + 1) * half], *ring_facts(cols, way)) for k, way in enumerate((1, -1))]
    held = [w[1] for w in ways]
    for step in range(1, cols):
        for k, (way, _, perm, owner) in enumerate(ways):
            held[k] = lax.ppermute(held[k], "col", perm)
        for k, (way, _, perm, owner) in enumerate(ways):
            full = lax.dynamic_update_slice(full, held[k], (owner(step) * 2 * half + k * half, 0))
    return full


def ring_scatter(array, cols):
    size = array.shape[0] // cols
    half = size // 2
    sums = []
    for k, way in enumerate((1, -1)):
        perm, owner = ring_facts(cols, way)
        mine = lambda back: lax.dynamic_slice(array, (owner(back) * size + k * half, 0), (half, array.shape[1]))
        held = mine(1)
        for step in range(1, cols):
            held = lax.ppermute(held, "col", perm)
            held = held + mine(step + 1)
        sums.append(held)
    return jnp.concatenate(sums, axis=0)


def pick(pieces, index):
    return lax.dynamic_index_in_dim(pieces, index, 0, keepdims=False)


def to_row(shard, rows, cols):
    ratio = cols // rows
    col = lax.axis_index("col")
    parts = shard.reshape(ratio, shard.shape[0] // ratio, shard.shape[1])
    got = []
    for k in range(ratio):
        perm = [
            (r * cols + c, (c // ratio) * cols + r * ratio + (c + k) % ratio)
            for r in range(rows) for c in range(cols)
        ]
        got.append(lax.ppermute(pick(parts, lax.rem(col + k, ratio)), ("row", "col"), perm))
    got = jnp.stack(got)
    return jnp.concatenate([pick(got, lax.rem(col + ratio - m, ratio)) for m in range(ratio)], axis=1)


def to_col(shard, rows, cols):
    ratio = cols // rows
    col = lax.axis_index("col")
    parts = jnp.stack(jnp.split(shard, ratio, axis=1))
    got = []
    for k in range(ratio):
        perm = [
            ((c // ratio) * cols + r * ratio + (c + k) % ratio, r * cols + c)
            for r in range(rows) for c in range(cols)
        ]
        got.append(lax.ppermute(pick(parts, lax.rem(col + ratio - k, ratio)), ("row", "col"), perm))
    got = jnp.stack(got)
    return jnp.concatenate([pick(got, lax.rem(m + ratio - lax.rem(col, ratio), ratio)) for m in range(ratio)], axis=0)


def shards(rows, cols, amplitudes, integrals, factors, occ_energy, vir_energy):
    oi, oj, vir, _ = amplitudes.shape
    parts = 2 if oi % 2 == 0 else 1
    pieces = 4
    wide = oi // parts * vir
    own = jnp.transpose(factors, (1, 0, 2)).reshape(factors.shape[1], oj * vir)
    fac_col = lax.all_gather(own, "row", axis=0, tiled=True)
    moved = to_row(own, rows, cols)
    fac_row = [ring_gather(moved[:, g * wide:(g + 1) * wide], cols) for g in range(parts)]
    left = []
    for g in range(parts):
        left.append(left_product(amplitudes, fac_col, g, parts))
    left = [ring_scatter(part, cols) for part in left]
    right = []
    for h in range(pieces):
        right.append(right_product(amplitudes, fac_row, rows, h, pieces))
    right = [lax.psum_scatter(piece, "row", scatter_dimension=0, tiled=True) for piece in right]
    right = jnp.concatenate(right, axis=0)
    across = to_row(right, rows, cols)
    summed = [2.0 * left[g] - across[:, g * wide:(g + 1) * wide] for g in range(parts)]
    back = 2.0 * to_col(jnp.concatenate(left, axis=1), rows, cols) - right
    sum_col = lax.all_gather(back, "row", axis=0, tiled=True)
    sum_row = [ring_gather(part, cols) for part in summed]
    occ_left = lax.dynamic_slice_in_dim(occ_energy, lax.axis_index("row") * oi, oi)
    occ_right = lax.dynamic_slice_in_dim(occ_energy, lax.axis_index("col") * oj, oj)
    out = None
    for g in range(parts):
        out = base(integrals, fac_row[g], sum_col, g, parts, out)
    for g in range(parts):
        out = final(out, sum_row[g], fac_col, occ_left, occ_right, vir_energy, g, parts)
    return out


def solution(mesh):
    cols = mesh.shape["col"]
    return jax.shard_map(
        functools.partial(shards, mesh.shape["row"], cols),
        mesh=mesh,
        in_specs=(
            P("row", "col", None, None),
            P("row", "col", None, None),
            P("col", "row", None),
            P(),
            P(),
        ),
        out_specs=P("row", "col", None, None),
        check_vma=False,
    )
```
